256 devices in a mesh: seq: 32 (over z, y), tp: 8 (over x, core).
Axes of the slice: x: 4, y: 4, z: 8, core: 2. Of those that a mesh axis runs over, the one named last changes fastest.
Arguments:
- query: bfloat16 [16384, 8192], P('seq', 'tp'), may hold values from -6 to 6
- key: bfloat16 [16384, 8192], P('seq', 'tp'), may hold values from -6 to 6
- value: bfloat16 [16384, 8192], P('seq', 'tp'), may hold values from -6 to 6
- gain: float32 [8192], P('tp'), may hold values from 0.1 to 1.9
- cotangent: bfloat16 [16384, 8192], P('seq', 'tp'), may hold values from -24 to 24
Outputs:
- normed: bfloat16 [16384, 8192], P('seq', 'tp')
- grad_query: bfloat16 [16384, 8192], P('seq', 'tp')
- grad_key: bfloat16 [16384, 8192], P('seq', 'tp')
- grad_value: bfloat16 [16384, 8192], P('seq', 'tp')
- grad_gain: float32 [8192], P('tp')
The draws below stay inside these ranges and needn't reach their ends.
All inputs are finite; a program needn't handle non-finite values.
Results may differ from the reference program's by a relative error of at most 0.013.
Values may be sent and summed in bfloat16 or wider, within the bound.
No kernel may reach another device: no remote copies, remote signals or barrier semaphores. Data moves between devices by JAX's collectives and lax.ppermute only.
A program may use at most 128 MiB of HBM per device.

```python
import jax
import jax.numpy as jnp
from jax import lax

HEADS = 64
HD = 128
TOK_DEV = 512
TOKENS = 16384
WIDTH = 8192
N_SEQ = 32


def draw_cotangent(key, part):
    position = jnp.arange(TOKENS, dtype=jnp.float32)
    scales = 1.0 + 2.0 * position / TOKENS
    noise = jax.random.normal(key, (TOKENS, HEADS * HD), jnp.float32)
    return jnp.clip(noise * scales[:, None], -24.0, 24.0).astype(jnp.bfloat16)


def block_levels(own_key, shape, pieces, low, top_value):
    level, own = 1.0, jax.random.fold_in(own_key, 6)
    for dim, parts in pieces:
        heights = jnp.exp(jax.random.uniform(jax.random.fold_in(own, dim), (parts,), jnp.float32, low / len(pieces), top_value / len(pieces)))
        level = level * jnp.repeat(heights, shape[dim] // parts).reshape([-1 if axis == dim else 1 for axis in range(len(shape))])
    return level


def normal_values(key, dims, deviation, most, cuts=(), held_as=jnp.bfloat16):
    array = jax.random.normal(key, dims, jnp.float32) * deviation
    if len(cuts) > 0:
        array = block_levels(key, dims, cuts, -0.22, 0.18) * array
    return jnp.clip(array, min=-most, max=most).astype(held_as)


def setup_inputs(seed: int = 0) -> dict:
    splits = jax.random.split(jax.random.key(seed), 6)
    return {
        "query": normal_values(splits[0], (TOKENS, WIDTH), 1.0, 6.0, ((0, 32), (1, 8))),
        "key": normal_values(splits[1], (TOKENS, WIDTH), 1.0, 6.0, ((0, 32), (1, 8))),
        "value": normal_values(splits[2], (TOKENS, WIDTH), 1.0, 6.0, ((0, 32), (1, 8))),
        "gain": jnp.clip(1.0 + 0.18 * jax.random.normal(splits[3], (WIDTH,), jnp.float32), 0.1, 1.9),
        "cotangent": draw_cotangent(jax.random.fold_in(splits[5], 71), 0),
    }


epsilon = 1e-06

def reference(query, key, value, gain, cotangent):
    groups = N_SEQ
    full_width = HEADS * HD
    shape_four = (groups, TOK_DEV, HEADS, HD)
    queries = query.reshape(shape_four)
    keys_all = key.reshape(shape_four)
    values_all = value.reshape(shape_four)
    grads_in = cotangent.reshape(groups, TOK_DEV, full_width)
    causal = (jnp.arange(TOK_DEV)[:, None] >= jnp.arange(TOK_DEV)[None, :]).astype(jnp.float32)
    gain_full = gain.astype(jnp.float32)

    def local_state(pair):
        return jnp.einsum('thd,the->hde', pair[0].astype(jnp.float32), pair[1].astype(jnp.float32)).astype(jnp.bfloat16)
    state_low = lax.map(local_state, (keys_all, values_all))
    zero_state = jnp.zeros((1, HEADS, HD, HD), jnp.float32)
    running = jnp.cumsum(state_low.astype(jnp.float32), axis=0)
    prefix_low = jnp.concatenate([zero_state, running[:-1]], 0).astype(jnp.bfloat16)

    def forward_group(items):
        group_query, group_key, group_value, group_grad, group_prefix = items
        query_f = group_query.astype(jnp.float32)
        key_f = group_key.astype(jnp.float32)
        value_f = group_value.astype(jnp.float32)
        prefix_f = group_prefix.astype(jnp.float32)
        scores = (jnp.einsum('thd,shd->hts', query_f, key_f) * causal[None]).astype(jnp.bfloat16)
        attended = jnp.einsum('hts,shd->thd', scores.astype(jnp.float32), value_f) + jnp.einsum('thd,hde->the', query_f, prefix_f)
        attended = attended.reshape(TOK_DEV, full_width)
        inverse = lax.rsqrt(lax.optimization_barrier(jnp.mean(attended * attended, axis=-1)) + epsilon)
        grad_f = group_grad.astype(jnp.float32)
        scaled_grad = grad_f * gain_full
        cross = lax.optimization_barrier(jnp.sum(attended * scaled_grad, axis=-1))
        normed = (attended * inverse[:, None] * gain_full).astype(jnp.bfloat16)
        grad_out = scaled_grad * inverse[:, None] - attended * (inverse ** 3 * cross / full_width)[:, None]
        grad_out = grad_out.astype(jnp.bfloat16).reshape(TOK_DEV, HEADS, HD)
        gain_part = lax.optimization_barrier(jnp.sum(grad_f * attended * inverse[:, None], axis=0))
        grad_f_out = grad_out.astype(jnp.float32)
        back_scores = (jnp.einsum('thd,shd->hts', grad_f_out, value_f) * causal[None]).astype(jnp.bfloat16)
        grad_q = jnp.einsum('hts,shd->thd', back_scores.astype(jnp.float32), key_f) + jnp.einsum('the,hde->thd', grad_f_out, prefix_f)
        block_grad = jnp.einsum('thd,the->hde', query_f, grad_f_out).astype(jnp.bfloat16)
        return (normed, grad_q.astype(jnp.bfloat16), grad_out, block_grad, gain_part)
    normed, grad_q, grad_outs, grad_low, gain_parts = lax.map(forward_group, (queries, keys_all, values_all, grads_in, prefix_low))
    running_back = jnp.cumsum(grad_low.astype(jnp.float32)[::-1], axis=0)[::-1]
    suffix_low = jnp.concatenate([running_back[1:], zero_state], 0).astype(jnp.bfloat16)

    def backward_group(items):
        group_query, group_key, group_value, group_out, group_suffix = items
        query_f = group_query.astype(jnp.float32)
        key_f = group_key.astype(jnp.float32)
        value_f = group_value.astype(jnp.float32)
        out_f = group_out.astype(jnp.float32)
        suffix_f = group_suffix.astype(jnp.float32)
        scores = (jnp.einsum('thd,shd->hts', query_f, key_f) * causal[None]).astype(jnp.bfloat16)
        back_scores = (jnp.einsum('thd,shd->hts', out_f, value_f) * causal[None]).astype(jnp.bfloat16)
        grad_k = jnp.einsum('hts,thd->shd', back_scores.astype(jnp.float32), query_f) + jnp.einsum('she,hde->shd', value_f, suffix_f)
        grad_v = jnp.einsum('hts,the->she', scores.astype(jnp.float32), out_f) + jnp.einsum('shd,hde->she', key_f, suffix_f)
        return (grad_k.astype(jnp.bfloat16), grad_v.astype(jnp.bfloat16))
    grad_k, grad_v = lax.map(backward_group, (queries, keys_all, values_all, grad_outs, suffix_low))
    flat = (TOKENS, full_width)
    return (normed.reshape(flat), grad_q.reshape(flat), grad_k.reshape(flat), grad_v.reshape(flat), lax.optimization_barrier(jnp.sum(gain_parts, axis=0)))
```

```python
import functools

import jax
import jax.numpy as jnp
from jax import lax
from jax.experimental import pallas as pl
from jax.experimental.pallas import tpu as pltpu
from jax.sharding import PartitionSpec as P

HD = 128
EPSILON = 1e-06
GAIN_ROWS = 8
F32, BF16 = jnp.float32, jnp.bfloat16


def dot(a, b, contract_a, contract_b):
    return lax.dot_general(
        a, b, (((contract_a,), (contract_b,)), ((), ())), preferred_element_type=F32
    )


def causal(rows):
    t = lax.broadcasted_iota(jnp.int32, (rows, rows), 0)
    s = lax.broadcasted_iota(jnp.int32, (rows, rows), 1)
    return t >= s


def head(ref, i):
    return ref[:, i * HD : (i + 1) * HD]


def lower_product(a, b, x):
    half = a.shape[0] // 2
    mask = causal(half)
    first, last = slice(0, half), slice(half, None)
    s00 = jnp.where(mask, dot(a[first], b[first], 1, 1), 0.0).astype(BF16)
    s10 = dot(a[last], b[first], 1, 1).astype(BF16)
    s11 = jnp.where(mask, dot(a[last], b[last], 1, 1), 0.0).astype(BF16)
    return dot(s00, x[first], 1, 0), dot(s10, x[first], 1, 0) + dot(s11, x[last], 1, 0)


def upper_product(a, b, x):
    half = a.shape[0] // 2
    s = lax.broadcasted_iota(jnp.int32, (half, half), 0)
    t = lax.broadcasted_iota(jnp.int32, (half, half), 1)
    mask = t >= s
    first, last = slice(0, half), slice(half, None)
    s00 = jnp.where(mask, dot(a[first], b[first], 1, 1), 0.0).astype(BF16)
    s01 = dot(a[first], b[last], 1, 1).astype(BF16)
    s11 = jnp.where(mask, dot(a[last], b[last], 1, 1), 0.0).astype(BF16)
    return dot(s00, x[first], 1, 0) + dot(s01, x[last], 1, 0), dot(s11, x[last], 1, 0)


def three_parts(x):
    high = x.astype(BF16).astype(F32)
    rest = x - high
    middle = rest.astype(BF16).astype(F32)
    return high, middle, rest - middle


def gain_tile(x):
    row = lax.broadcasted_iota(jnp.int32, (GAIN_ROWS, HD), 0)
    high, middle, low = (jnp.broadcast_to(p, (GAIN_ROWS, HD)) for p in three_parts(x))
    tile = jnp.where(row == 0, high, jnp.where(row == 1, middle, jnp.where(row == 2, low, 0.0)))
    return tile.astype(BF16)


def state_kernel(key, value, out):
    heads = key.shape[1] // HD
    per_head = out.shape[0] // heads
    for i in range(heads):
        state = dot(head(key, i), head(value, i), 0, 0).astype(BF16)
        out[i * per_head : (i + 1) * per_head] = state.reshape(per_head, -1, HD)


def before_kernel(states, out):
    total = jnp.zeros(states.shape[1:], F32)
    for j in range(states.shape[0]):
        out[j] = total.astype(BF16)
        total += states[j].astype(F32)


def after_kernel(states, out):
    devices = states.shape[0]
    rows = states.shape[1] - GAIN_ROWS
    total = jnp.zeros((rows, HD), F32)
    gain = jnp.zeros((GAIN_ROWS, HD), F32)
    for j in reversed(range(devices)):
        out[j, :rows] = total.astype(BF16)
        total += states[j, :rows].astype(F32)
        gain += states[j, rows:].astype(F32)
    tile = gain_tile(jnp.sum(gain, axis=0, keepdims=True))
    for j in range(devices):
        out[j, rows:] = tile


def intra_kernel(query, key, value, out):
    half = query.shape[0] // 2
    for i in range(query.shape[1] // HD):
        top, bottom = lower_product(head(query, i), head(key, i), head(value, i))
        out[:half, i * HD : (i + 1) * HD] = top
        out[half:, i * HD : (i + 1) * HD] = bottom


def attend_kernel(intra, query, prefix, cotangent, gain, attended, sums, squares, cross):
    step = pl.program_id(0)

    @pl.when(step == 0)
    def _():
        squares[...] = jnp.zeros_like(squares)
        cross[...] = jnp.zeros_like(cross)

    heads = query.shape[1] // HD
    per_head = prefix.shape[0] // heads
    sq, cr = squares[...], cross[...]
    for i in range(heads):
        state = prefix[i * per_head : (i + 1) * per_head].reshape(HD, HD)
        att = head(intra, i) + dot(head(query, i), state, 1, 0)
        attended[:, i * HD : (i + 1) * HD] = att
        scaled = head(cotangent, i).astype(F32) * head(gain, i)
        sq += att * att
        cr += att * scaled
    squares[...] = sq
    cross[...] = cr

    @pl.when(step == pl.num_programs(0) - 1)
    def _():
        parts = squares.shape[0] // HD
        for n, ref in enumerate((squares, cross)):
            row = jnp.sum(ref[...].T, axis=0, keepdims=True)
            for i in range(parts):
                part = row[:, i * HD : (i + 1) * HD]
                sums[:, n * parts + i, :] = jnp.broadcast_to(part, (sums.shape[0], HD))


def row_factors(sums, full_width):
    total = jnp.sum(sums[...], axis=0)
    parts = total.shape[0] // 2
    inverse, other = [], []
    for i in range(parts):
        sq, cr = total[i : i + 1], total[parts + i : parts + i + 1]
        inv = lax.rsqrt(sq / full_width + EPSILON)
        inverse.append(jnp.broadcast_to(inv, (HD, HD)).T)
        other.append(jnp.broadcast_to(inv * inv * inv * cr / full_width, (HD, HD)).T)
    return jnp.concatenate(inverse, 0), jnp.concatenate(other, 0)


def out_grad_kernel(full_width, sums, attended, cotangent, query, gain, out, inverse, other):
    @pl.when(pl.program_id(0) == 0)
    def _():
        inverse[...], other[...] = row_factors(sums, full_width)

    heads = query.shape[1] // HD
    per_head = out.shape[0] // heads
    rows = out.shape[1] - GAIN_ROWS
    inv, oth = inverse[...], other[...]
    for i in range(heads):
        att, cot = head(attended, i), head(cotangent, i).astype(F32)
        grad = (cot * head(gain, i) * inv - att * oth).astype(BF16)
        state = dot(head(query, i), grad, 0, 0).astype(BF16)
        here = slice(i * per_head, (i + 1) * per_head)
        out[here, :rows] = state.reshape(per_head, rows, HD)
        tile = gain_tile(jnp.sum(cot * att * inv, axis=0, keepdims=True))
        out[here, rows:] = jnp.broadcast_to(tile[None], (per_head, GAIN_ROWS, HD))


def back_kernel(
    full_width, sums, attended, cotangent, query, key, value, prefix, gain,
    normed, grad_query, key_part, value_part, inverse, other,
):
    @pl.when(pl.program_id(0) == 0)
    def _():
        inverse[...], other[...] = row_factors(sums, full_width)

    heads = query.shape[1] // HD
    per_head = prefix.shape[0] // heads
    half = query.shape[0] // 2
    inv, oth = inverse[...], other[...]
    for i in range(heads):
        here = slice(i * HD, (i + 1) * HD)
        att, gains = head(attended, i), head(gain, i)
        q, k, v = head(query, i), head(key, i), head(value, i)
        normed[:, here] = (att * inv * gains).astype(BF16)
        grad = (head(cotangent, i).astype(F32) * gains * inv - att * oth).astype(BF16)
        state = prefix[i * per_head : (i + 1) * per_head].reshape(HD, HD)
        across = dot(grad, state, 1, 1)
        top, bottom = lower_product(grad, v, k)
        grad_query[:half, here] = (top + across[:half]).astype(BF16)
        grad_query[half:, here] = (bottom + across[half:]).astype(BF16)
        top, bottom = upper_product(v, grad, q)
        key_part[:half, here] = top
        key_part[half:, here] = bottom
        top, bottom = upper_product(k, q, grad)
        value_part[:half, here] = top
        value_part[half:, here] = bottom


def last_kernel(key_part, value_part, key, value, suffix, grad_key, grad_value, grad_gain):
    heads = key.shape[1] // HD
    per_head = suffix.shape[0] // heads
    rows = suffix.shape[1] - GAIN_ROWS
    for i in range(heads):
        here = slice(i * HD, (i + 1) * HD)
        state = suffix[i * per_head : (i + 1) * per_head, :rows].reshape(HD, HD)
        grad_key[:, here] = (head(key_part, i) + dot(head(value, i), state, 1, 1)).astype(BF16)
        grad_value[:, here] = (head(value_part, i) + dot(head(key, i), state, 1, 0)).astype(BF16)
        tile = suffix[i * per_head, rows:].astype(F32)
        grad_gain[:, here] = jnp.sum(tile, axis=0, keepdims=True)


def local(query, key, value, gain, cotangent):
    rows, width = query.shape
    heads = width // HD
    tp, devices = lax.axis_size("tp"), lax.axis_size("seq")
    full_width = tp * width
    piece = width // devices
    gain = gain.reshape(1, width)

    def call(kernel, name, inputs, outputs, per_step, flops=0, scratch=()):
        steps = heads // per_step

        def spec(array, cut):
            shape = list(array.shape)
            if cut is None:
                return pl.BlockSpec(tuple(shape), lambda i: (0,) * len(shape))
            shape[cut] //= steps
            return pl.BlockSpec(
                tuple(shape), lambda i: tuple(i if d == cut else 0 for d in range(len(shape)))
            )

        arrays = [a for a, _ in inputs]
        bytes_moved = sum(a.size * a.dtype.itemsize for a in arrays + [o for o, _ in outputs])
        return pl.pallas_call(
            kernel,
            grid=(steps,),
            in_specs=[spec(*i) for i in inputs],
            out_specs=[spec(*o) for o in outputs],
            out_shape=[o for o, _ in outputs],
            scratch_shapes=list(scratch),
            compiler_params=pltpu.CompilerParams(
                dimension_semantics=("arbitrary",), vmem_limit_bytes=24 << 20
            ),
            cost_estimate=pl.CostEstimate(
                flops=flops, bytes_accessed=bytes_moved, transcendentals=0
            ),
            name=name,
        )(*arrays)

    shape = jax.ShapeDtypeStruct
    states = shape((devices, piece, HD), BF16)
    more_states = shape((devices, piece + GAIN_ROWS, HD), BF16)
    wide = shape((rows, width), F32)
    narrow = shape((rows, width), BF16)
    vectors = [pltpu.VMEM((rows, HD), F32)] * 2
    state_flops = 2 * rows * HD * width
    block_flops = 2 * rows * rows * width * 3 // 4

    (state,) = call(state_kernel, "state", [(key, 1), (value, 1)], [(states, 0)], 2, state_flops)
    state = lax.all_to_all(state, "seq", 0, 0, tiled=True)
    (intra,) = call(
        intra_kernel, "intra", [(query, 1), (key, 1), (value, 1)], [(wide, 1)], 1, 2 * block_flops
    )
    (prefix,) = call(before_kernel, "before", [(state, None)], [(states, None)], heads)
    prefix = lax.all_to_all(prefix, "seq", 0, 0, tiled=True)
    attended, sums = call(
        attend_kernel, "attend",
        [(intra, 1), (query, 1), (prefix, 0), (cotangent, 1), (gain, 1)],
        [(wide, 1), (shape((tp, 2 * rows // HD, HD), F32), None)],
        2, state_flops, vectors,
    )
    sums = lax.all_to_all(sums, "tp", 0, 0, tiled=True)
    (grad_state,) = call(
        functools.partial(out_grad_kernel, full_width), "out_grad",
        [(sums, None), (attended, 1), (cotangent, 1), (query, 1), (gain, 1)],
        [(more_states, 0)],
        2, state_flops, vectors,
    )
    grad_state = lax.all_to_all(grad_state, "seq", 0, 0, tiled=True)
    normed, grad_query, key_part, value_part = call(
        functools.partial(back_kernel, full_width), "back",
        [(sums, None), (attended, 1), (cotangent, 1), (query, 1), (key, 1), (value, 1),
         (prefix, 0), (gain, 1)],
        [(narrow, 1), (narrow, 1), (wide, 1), (wide, 1)],
        1, 6 * block_flops + state_flops, vectors,
    )
    (suffix,) = call(after_kernel, "after", [(grad_state, None)], [(more_states, None)], heads)
    suffix = lax.all_to_all(suffix, "seq", 0, 0, tiled=True)
    grad_key, grad_value, grad_gain = call(
        last_kernel, "last",
        [(key_part, 1), (value_part, 1), (key, 1), (value, 1), (suffix, 0)],
        [(narrow, 1), (narrow, 1), (shape((1, width), F32), 1)],
        2, 2 * state_flops,
    )
    return normed, grad_query, grad_key, grad_value, grad_gain.reshape(width)


def solution(mesh):
    block = P("seq", "tp")
    return jax.shard_map(
        local,
        mesh=mesh,
        in_specs=(block, block, block, P("tp"), block),
        out_specs=(block, block, block, block, P("tp")),
        check_vma=False,
    )
```

```python
import functools

import jax
import jax.numpy as jnp
from jax import lax
from jax.experimental import pallas as pl
from jax.experimental.pallas import tpu as pltpu
from jax.sharding import PartitionSpec as P


HD = 128
EPSILON = 1e-06
GAIN_ROWS = 8
F32, BF16 = jnp.float32, jnp.bfloat16


def dot(a, b, contract_a, contract_b):
    return lax.dot_general(
        a, b, (((contract_a,), (contract_b,)), ((), ())), preferred_element_type=F32
    )


def causal(rows):
    t = lax.broadcasted_iota(jnp.int32, (rows, rows), 0)
    s = lax.broadcasted_iota(jnp.int32, (rows, rows), 1)
    return t >= s


def head(ref, i):
    return ref[:, i * HD : (i + 1) * HD]


def lower_product(a, b, x):
    half = a.shape[0] // 2
    mask = causal(half)
    first, last = slice(0, half), slice(half, None)
    s00 = jnp.where(mask, dot(a[first], b[first], 1, 1), 0.0).astype(BF16)
    s10 = dot(a[last], b[first], 1, 1).astype(BF16)
    s11 = jnp.where(mask, dot(a[last], b[last], 1, 1), 0.0).astype(BF16)
    return dot(s00, x[first], 1, 0), dot(s10, x[first], 1, 0) + dot(s11, x[last], 1, 0)


def upper_product(a, b, x):
    half = a.shape[0] // 2
    s = lax.broadcasted_iota(jnp.int32, (half, half), 0)
    t = lax.broadcasted_iota(jnp.int32, (half, half), 1)
    mask = t >= s
    first, last = slice(0, half), slice(half, None)
    s00 = jnp.where(mask, dot(a[first], b[first], 1, 1), 0.0).astype(BF16)
    s01 = dot(a[first], b[last], 1, 1).astype(BF16)
    s11 = jnp.where(mask, dot(a[last], b[last], 1, 1), 0.0).astype(BF16)
    return dot(s00, x[first], 1, 0) + dot(s01, x[last], 1, 0), dot(s11, x[last], 1, 0)


def three_parts(x):
    high = x.astype(BF16).astype(F32)
    rest = x - high
    middle = rest.astype(BF16).astype(F32)
    return high, middle, rest - middle


def gain_tile(x):
    row = lax.broadcasted_iota(jnp.int32, (GAIN_ROWS, HD), 0)
    high, middle, low = (jnp.broadcast_to(p, (GAIN_ROWS, HD)) for p in three_parts(x))
    tile = jnp.where(row == 0, high, jnp.where(row == 1, middle, jnp.where(row == 2, low, 0.0)))
    return tile.astype(BF16)


def state_kernel(key, value, out, keys, values, total, arrived):
    chunks = keys.shape[0]
    rows = keys.shape[1]
    heads = key.shape[1] // HD
    per_head = out.shape[0] // heads

    def copies(c):
        here = pl.ds(c * rows, rows)
        return (
            pltpu.make_async_copy(key.at[here], keys.at[c], arrived.at[0, c]),
            pltpu.make_async_copy(value.at[here], values.at[c], arrived.at[1, c]),
        )

    for c in range(chunks):
        for copy in copies(c):
            copy.start()
    for c in range(chunks):
        for copy in copies(c):
            copy.wait()
        for i in range(heads):
            here = slice(i * HD, (i + 1) * HD)
            state = dot(keys[c, :, here], values[c, :, here], 0, 0)
            if c > 0:
                state += total[i]
            if c < chunks - 1:
                total[i] = state
            else:
                out[i * per_head : (i + 1) * per_head] = state.astype(BF16).reshape(
                    per_head, -1, HD
                )


def before_kernel(states, out):
    total = jnp.zeros(states.shape[1:], F32)
    for j in range(states.shape[0]):
        out[j] = total.astype(BF16)
        total += states[j].astype(F32)


def after_kernel(states, out):
    devices = states.shape[0]
    rows = states.shape[1] - GAIN_ROWS
    total = jnp.zeros((rows, HD), F32)
    gain = jnp.zeros((GAIN_ROWS, HD), F32)
    for j in reversed(range(devices)):
        out[j, :rows] = total.astype(BF16)
        total += states[j, :rows].astype(F32)
        gain += states[j, rows:].astype(F32)
    tile = gain_tile(jnp.sum(gain, axis=0, keepdims=True))
    for j in range(devices):
        out[j, rows:] = tile


def intra_kernel(query, key, value, out):
    half = query.shape[0] // 2
    for i in range(query.shape[1] // HD):
        top, bottom = lower_product(head(query, i), head(key, i), head(value, i))
        out[:half, i * HD : (i + 1) * HD] = top
        out[half:, i * HD : (i + 1) * HD] = bottom


def attend_kernel(intra, query, prefix, cotangent, gain, attended, grads_in, sums, arrived):
    rows = query.shape[0]
    heads = query.shape[1] // HD
    per_head = prefix.shape[0] // heads
    copy = pltpu.make_async_copy(cotangent, grads_in, arrived)
    copy.start()
    squares = jnp.zeros((rows, HD), F32)
    cross = jnp.zeros((rows, HD), F32)
    for i in range(heads):
        state = prefix[i * per_head : (i + 1) * per_head].reshape(HD, HD)
        att = head(intra, i) + dot(head(query, i), state, 1, 0)
        attended[:, i * HD : (i + 1) * HD] = att
        squares += att * att
    copy.wait()
    for i in range(heads):
        cross += head(attended, i) * (head(grads_in, i).astype(F32) * head(gain, i))
    parts = rows // HD
    for n, x in enumerate((squares, cross)):
        row = jnp.sum(x.T, axis=0, keepdims=True)
        for i in range(parts):
            part = row[:, i * HD : (i + 1) * HD]
            sums[:, n * parts + i, :] = jnp.broadcast_to(part, (sums.shape[0], HD))


def row_factors(sums, full_width):
    total = jnp.sum(sums[...], axis=0)
    parts = total.shape[0] // 2
    inverse, other = [], []
    for i in range(parts):
        sq, cr = total[i : i + 1], total[parts + i : parts + i + 1]
        inv = lax.rsqrt(sq / full_width + EPSILON)
        inverse.append(jnp.broadcast_to(inv, (HD, HD)).T)
        other.append(jnp.broadcast_to(inv * inv * inv * cr / full_width, (HD, HD)).T)
    return jnp.concatenate(inverse, 0), jnp.concatenate(other, 0)


def out_grad_kernel(full_width, sums, attended, cotangent, query, gain, out, again, sent):
    copy = pltpu.make_async_copy(attended, again, sent)
    copy.start()
    heads = query.shape[1] // HD
    per_head = out.shape[0] // heads
    rows = out.shape[1] - GAIN_ROWS
    inv, oth = row_factors(sums, full_width)
    for i in range(heads):
        att, cot = head(attended, i), head(cotangent, i).astype(F32)
        grad = (cot * head(gain, i) * inv - att * oth).astype(BF16)
        state = dot(head(query, i), grad, 0, 0).astype(BF16)
        here = slice(i * per_head, (i + 1) * per_head)
        out[here, :rows] = state.reshape(per_head, rows, HD)
        tile = gain_tile(jnp.sum(cot * att * inv, axis=0, keepdims=True))
        out[here, rows:] = jnp.broadcast_to(tile[None], (per_head, GAIN_ROWS, HD))
    copy.wait()


def query_kernel(
    full_width, sums, attended, cotangent, key, value, prefix, gain,
    normed, grads, grad_query, inverse, other,
):
    @pl.when(pl.program_id(0) == 0)
    def _():
        inverse[...], other[...] = row_factors(sums, full_width)

    heads = key.shape[1] // HD
    per_head = prefix.shape[0] // heads
    half = key.shape[0] // 2
    inv, oth = inverse[...], other[...]
    for i in range(heads):
        here = slice(i * HD, (i + 1) * HD)
        att, gains = head(attended, i), head(gain, i)
        normed[:, here] = (att * inv * gains).astype(BF16)
        grad = (head(cotangent, i).astype(F32) * gains * inv - att * oth).astype(BF16)
        grads[:, here] = grad
        state = prefix[i * per_head : (i + 1) * per_head].reshape(HD, HD)
        across = dot(grad, state, 1, 1)
        top, bottom = lower_product(grad, head(value, i), head(key, i))
        grad_query[:half, here] = (top + across[:half]).astype(BF16)
        grad_query[half:, here] = (bottom + across[half:]).astype(BF16)


def key_value_kernel(grads, query, key, value, key_part, value_part):
    half = key.shape[0] // 2
    for i in range(key.shape[1] // HD):
        here = slice(i * HD, (i + 1) * HD)
        grad, q = head(grads, i), head(query, i)
        top, bottom = upper_product(head(value, i), grad, q)
        key_part[:half, here] = top.astype(BF16)
        key_part[half:, here] = bottom.astype(BF16)
        top, bottom = upper_product(head(key, i), q, grad)
        value_part[:half, here] = top.astype(BF16)
        value_part[half:, here] = bottom.astype(BF16)


def last_kernel(
    key_part, value_part, key, value, suffix, grad_key, grad_value, grad_gain,
    parts, results, arrived, sent,
):
    heads = key.shape[1] // HD
    per_head = suffix.shape[0] // heads
    state_rows = suffix.shape[1] - GAIN_ROWS
    _, cuts, rows, _ = parts.shape

    def reads(c):
        here = pl.ds(c * rows, rows)
        return [
            pltpu.make_async_copy(a.at[here], parts.at[n, c], arrived.at[n, c])
            for n, a in enumerate((key_part, value_part))
        ]

    def writes(c):
        here = pl.ds(c * rows, rows)
        return [
            pltpu.make_async_copy(results.at[n, c], a.at[here], sent.at[n, c])
            for n, a in enumerate((grad_key, grad_value))
        ]

    for c in range(cuts):
        for copy in reads(c):
            copy.start()
    for i in range(heads):
        tile = suffix[i * per_head, state_rows:].astype(F32)
        grad_gain[:, i * HD : (i + 1) * HD] = jnp.sum(tile, axis=0, keepdims=True)
    for c in range(cuts):
        here = slice(c * rows, (c + 1) * rows)
        for copy in reads(c):
            copy.wait()
        for i in range(heads):
            columns = slice(i * HD, (i + 1) * HD)
            state = suffix[i * per_head : (i + 1) * per_head, :state_rows].reshape(HD, HD)
            from_key = dot(value[here, columns], state, 1, 1)
            from_value = dot(key[here, columns], state, 1, 0)
            for n, x in enumerate((from_key, from_value)):
                results[n, c, :, columns] = (parts[n, c, :, columns].astype(F32) + x).astype(BF16)
        for copy in writes(c):
            copy.start()
    for c in range(cuts):
        for copy in writes(c):
            copy.wait()


def exchange(array, axis):
    return lax.all_to_all(array, axis, 0, 0, tiled=True)


def layer(query, key, value, gain, cotangent):
    rows, width = query.shape
    heads = width // HD
    tp, devices = lax.axis_size("tp"), lax.axis_size("seq")
    full_width = tp * width
    piece = width // devices
    gain = gain.reshape(1, width)

    def call(kernel, inputs, outputs, steps, flops=0, scratch=(), mib=60):
        def spec(array, cut):
            shape = list(array.shape)
            if cut == "hbm":
                return pl.BlockSpec(memory_space=pltpu.HBM)
            if isinstance(cut, tuple):
                cut = cut[1]
            if not steps:
                return pl.BlockSpec(memory_space=pltpu.VMEM)
            if cut is None:
                return pl.BlockSpec(tuple(shape), lambda i: (0,) * len(shape))
            shape[cut] //= steps
            return pl.BlockSpec(
                tuple(shape), lambda i: tuple(i if d == cut else 0 for d in range(len(shape)))
            )

        def space(cut):
            name = cut[0] if isinstance(cut, tuple) else cut
            return {"hbm": pltpu.HBM, "vmem": pltpu.VMEM}.get(name)

        arrays = [
            pltpu.with_memory_space_constraint(a, space(cut)) if space(cut) else a
            for a, cut in inputs
        ]
        bytes_moved = sum(a.size * a.dtype.itemsize for a in arrays + [o for o, _ in outputs])
        return pl.pallas_call(
            kernel,
            grid=(steps,) if steps else (),
            in_specs=[spec(*i) for i in inputs],
            out_specs=[spec(*o) for o in outputs],
            out_shape=[
                space(cut)(o.shape, o.dtype) if space(cut) else o for o, cut in outputs
            ],
            scratch_shapes=list(scratch),
            compiler_params=pltpu.CompilerParams(vmem_limit_bytes=mib << 20),
            cost_estimate=pl.CostEstimate(
                flops=flops, bytes_accessed=bytes_moved, transcendentals=0
            ),
        )(*arrays)

    shape = jax.ShapeDtypeStruct
    states = shape((devices, piece, HD), BF16)
    more_states = shape((devices, piece + GAIN_ROWS, HD), BF16)
    wide = shape((rows, width), F32)
    narrow = shape((rows, width), BF16)
    vectors = [pltpu.VMEM((rows, HD), F32)] * 2
    state_flops = 2 * rows * HD * width
    block_flops = 2 * rows * rows * width * 3 // 4

    chunks = 4
    (state,) = call(
        state_kernel, [(key, "hbm"), (value, "hbm")], [(states, None)], 0, state_flops,
        [pltpu.VMEM((chunks, rows // chunks, width), BF16)] * 2
        + [pltpu.VMEM((heads, HD, HD), F32), pltpu.SemaphoreType.DMA((2, chunks))],
    )
    state = exchange(state, "seq")
    (intra,) = call(
        intra_kernel, [(query, 1), (key, 1), (value, 1)], [(wide, ("vmem", 1))],
        heads, 2 * block_flops,
    )
    (prefix,) = call(before_kernel, [(state, None)], [(states, None)], 0, mib=24)
    prefix = exchange(prefix, "seq")
    attended, grads_in, sums = call(
        attend_kernel,
        [(intra, None), (query, None), (prefix, None), (cotangent, "hbm"), (gain, None)],
        [(wide, None), (narrow, ("vmem", None)), (shape((tp, 2 * rows // HD, HD), F32), None)],
        0, state_flops, [pltpu.SemaphoreType.DMA], mib=24,
    )
    sums = exchange(sums, "tp")
    grad_state, again = call(
        functools.partial(out_grad_kernel, full_width),
        [(sums, None), (attended, None), (grads_in, None), (query, None), (gain, None)],
        [(more_states, None), (wide, "hbm")], 0, state_flops,
        [pltpu.SemaphoreType.DMA], mib=24,
    )
    grad_state = exchange(grad_state, "seq")
    normed, grads, grad_query = call(
        functools.partial(query_kernel, full_width),
        [(sums, None), (again, 1), (cotangent, 1), (key, 1), (value, 1), (prefix, 0), (gain, 1)],
        [(narrow, 1), (narrow, 1), (narrow, 1)],
        heads, 2 * block_flops + state_flops, vectors,
    )
    (suffix,) = call(
        after_kernel, [(grad_state, None)],
        [(more_states, None)], 0, mib=48,
    )
    key_part, value_part = call(
        key_value_kernel,
        [(grads, 1), (query, 1), (key, 1), (value, 1)],
        [(narrow, 1), (narrow, 1)],
        heads, 4 * block_flops,
    )
    suffix = exchange(suffix, "seq")
    cuts = 2
    grad_key, grad_value, grad_gain = call(
        last_kernel,
        [(key_part, "hbm"), (value_part, "hbm"), (key, None), (value, None), (suffix, None)],
        [(narrow, "hbm"), (narrow, "hbm"), (shape((1, width), F32), None)],
        0, 2 * state_flops,
        [pltpu.VMEM((2, cuts, rows // cuts, width), BF16)] * 2
        + [pltpu.SemaphoreType.DMA((2, cuts))] * 2,
        mib=44,
    )
    return normed, grad_query, grad_key, grad_value, grad_gain.reshape(width)


def solution(mesh):
    block = P("seq", "tp")
    return jax.shard_map(
        layer,
        mesh=mesh,
        in_specs=(block, block, block, P("tp"), block),
        out_specs=(block, block, block, block, P("tp")),
        check_vma=False,
    )
```

```python
import functools

import jax
import jax.numpy as jnp
from jax import lax
from jax.experimental import pallas as pl
from jax.experimental.pallas import tpu as pltpu
from jax.sharding import PartitionSpec as P


HD = 128
EPSILON = 1e-06
GAIN_ROWS = 8
F32, BF16 = jnp.float32, jnp.bfloat16


def dot(a, b, contract_a, contract_b):
    return lax.dot_general(
        a, b, (((contract_a,), (contract_b,)), ((), ())), preferred_element_type=F32
    )


def causal(rows):
    t = lax.broadcasted_iota(jnp.int32, (rows, rows), 0)
    s = lax.broadcasted_iota(jnp.int32, (rows, rows), 1)
    return t >= s


def head(ref, i):
    return ref[:, i * HD : (i + 1) * HD]


def lower_product(a, b, x):
    half = a.shape[0] // 2
    mask = causal(half)
    first, last = slice(0, half), slice(half, None)
    s00 = jnp.where(mask, dot(a[first], b[first], 1, 1), 0.0).astype(BF16)
    s10 = dot(a[last], b[first], 1, 1).astype(BF16)
    s11 = jnp.where(mask, dot(a[last], b[last], 1, 1), 0.0).astype(BF16)
    return dot(s00, x[first], 1, 0), dot(s10, x[first], 1, 0) + dot(s11, x[last], 1, 0)


def upper_product(a, b, x):
    half = a.shape[0] // 2
    s = lax.broadcasted_iota(jnp.int32, (half, half), 0)
    t = lax.broadcasted_iota(jnp.int32, (half, half), 1)
    mask = t >= s
    first, last = slice(0, half), slice(half, None)
    s00 = jnp.where(mask, dot(a[first], b[first], 1, 1), 0.0).astype(BF16)
    s01 = dot(a[first], b[last], 1, 1).astype(BF16)
    s11 = jnp.where(mask, dot(a[last], b[last], 1, 1), 0.0).astype(BF16)
    return dot(s00, x[first], 1, 0) + dot(s01, x[last], 1, 0), dot(s11, x[last], 1, 0)


def three_parts(x):
    high = x.astype(BF16).astype(F32)
    rest = x - high
    middle = rest.astype(BF16).astype(F32)
    return high, middle, rest - middle


def gain_tile(x):
    row = lax.broadcasted_iota(jnp.int32, (GAIN_ROWS, HD), 0)
    high, middle, low = (jnp.broadcast_to(p, (GAIN_ROWS, HD)) for p in three_parts(x))
    tile = jnp.where(row == 0, high, jnp.where(row == 1, middle, jnp.where(row == 2, low, 0.0)))
    return tile.astype(BF16)


def state_kernel(key, value, out, keys, values, total, arrived):
    chunks = keys.shape[0]
    rows = keys.shape[1]
    heads = key.shape[1] // HD
    per_head = out.shape[0] // heads

    def copies(c):
        here = pl.ds(c * rows, rows)
        return (
            pltpu.make_async_copy(key.at[here], keys.at[c], arrived.at[0, c]),
            pltpu.make_async_copy(value.at[here], values.at[c], arrived.at[1, c]),
        )

    for c in range(chunks):
        for copy in copies(c):
            copy.start()
    for c in range(chunks):
        for copy in copies(c):
            copy.wait()
        for i in range(heads):
            here = slice(i * HD, (i + 1) * HD)
            state = dot(keys[c, :, here], values[c, :, here], 0, 0)
            if c > 0:
                state += total[i]
            if c < chunks - 1:
                total[i] = state
            else:
                out[i * per_head : (i + 1) * per_head] = state.astype(BF16).reshape(
                    per_head, -1, HD
                )


def before_kernel(states, out):
    total = jnp.zeros(states.shape[1:], F32)
    for j in range(states.shape[0]):
        out[j] = total.astype(BF16)
        total += states[j].astype(F32)


def after_kernel(states, out):
    devices = states.shape[0]
    rows = states.shape[1] - GAIN_ROWS
    total = jnp.zeros((rows, HD), F32)
    gain = jnp.zeros((GAIN_ROWS, HD), F32)
    for j in reversed(range(devices)):
        out[j, :rows] = total.astype(BF16)
        total += states[j, :rows].astype(F32)
        gain += states[j, rows:].astype(F32)
    tile = gain_tile(jnp.sum(gain, axis=0, keepdims=True))
    for j in range(devices):
        out[j, rows:] = tile


def intra_kernel(query, key, value, out):
    half = query.shape[0] // 2
    for i in range(query.shape[1] // HD):
        top, bottom = lower_product(head(query, i), head(key, i), head(value, i))
        out[:half, i * HD : (i + 1) * HD] = top
        out[half:, i * HD : (i + 1) * HD] = bottom


def attend_kernel(intra, query, prefix, cotangent, gain, attended, grads_in, sums, arrived):
    rows = query.shape[0]
    heads = query.shape[1] // HD
    per_head = prefix.shape[0] // heads
    copy = pltpu.make_async_copy(cotangent, grads_in, arrived)
    copy.start()
    squares = jnp.zeros((rows, HD), F32)
    cross = jnp.zeros((rows, HD), F32)
    for i in range(heads):
        state = prefix[i * per_head : (i + 1) * per_head].reshape(HD, HD)
        att = head(intra, i) + dot(head(query, i), state, 1, 0)
        attended[:, i * HD : (i + 1) * HD] = att
        squares += att * att
    copy.wait()
    for i in range(heads):
        cross += head(attended, i) * (head(grads_in, i).astype(F32) * head(gain, i))
    parts = rows // HD
    for n, x in enumerate((squares, cross)):
        row = jnp.sum(x.T, axis=0, keepdims=True)
        for i in range(parts):
            part = row[:, i * HD : (i + 1) * HD]
            sums[:, n * parts + i, :] = jnp.broadcast_to(part, (sums.shape[0], HD))


def row_factors(sums, full_width):
    total = jnp.sum(sums[...], axis=0)
    parts = total.shape[0] // 2
    inverse, other = [], []
    for i in range(parts):
        sq, cr = total[i : i + 1], total[parts + i : parts + i + 1]
        inv = lax.rsqrt(sq / full_width + EPSILON)
        inverse.append(jnp.broadcast_to(inv, (HD, HD)).T)
        other.append(jnp.broadcast_to(inv * inv * inv * cr / full_width, (HD, HD)).T)
    return jnp.concatenate(inverse, 0), jnp.concatenate(other, 0)


def out_grad_kernel(full_width, sums, attended, cotangent, query, gain, out, again, sent):
    copy = pltpu.make_async_copy(attended, again, sent)
    copy.start()
    heads = query.shape[1] // HD
    per_head = out.shape[0] // heads
    rows = out.shape[1] - GAIN_ROWS
    inv, oth = row_factors(sums, full_width)
    for i in range(heads):
        att, cot = head(attended, i), head(cotangent, i).astype(F32)
        unit = cot * inv
        grad = (unit * head(gain, i) - att * oth).astype(BF16)
        state = dot(head(query, i), grad, 0, 0).astype(BF16)
        here = slice(i * per_head, (i + 1) * per_head)
        out[here, :rows] = state.reshape(per_head, rows, HD)
        tile = gain_tile(jnp.sum(unit * att, axis=0, keepdims=True))
        out[here, rows:] = jnp.broadcast_to(tile[None], (per_head, GAIN_ROWS, HD))
    copy.wait()


def query_kernel(
    full_width, sums, attended, cotangent, key, value, prefix, gain,
    normed, grads, grad_query, inverse, other,
):
    @pl.when(pl.program_id(0) == 0)
    def _():
        inverse[...], other[...] = row_factors(sums, full_width)

    heads = key.shape[1] // HD
    per_head = prefix.shape[0] // heads
    half = key.shape[0] // 2
    inv, oth = inverse[...], other[...]
    for i in range(heads):
        here = slice(i * HD, (i + 1) * HD)
        att, gains = head(attended, i), head(gain, i)
        normed[:, here] = (att * inv * gains).astype(BF16)
        grad = (head(cotangent, i).astype(F32) * inv * gains - att * oth).astype(BF16)
        grads[:, here] = grad
        state = prefix[i * per_head : (i + 1) * per_head].reshape(HD, HD)
        across = dot(grad, state, 1, 1)
        top, bottom = lower_product(grad, head(value, i), head(key, i))
        grad_query[:half, here] = (top + across[:half]).astype(BF16)
        grad_query[half:, here] = (bottom + across[half:]).astype(BF16)


def key_value_kernel(grads, query, key, value, key_part, value_part):
    half = key.shape[0] // 2
    for i in range(key.shape[1] // HD):
        here = slice(i * HD, (i + 1) * HD)
        grad, q = head(grads, i), head(query, i)
        top, bottom = upper_product(head(value, i), grad, q)
        key_part[:half, here] = top.astype(BF16)
        key_part[half:, here] = bottom.astype(BF16)
        top, bottom = upper_product(head(key, i), q, grad)
        value_part[:half, here] = top.astype(BF16)
        value_part[half:, here] = bottom.astype(BF16)


def last_kernel(
    key_part, value_part, key, value, suffix, grad_key, grad_value, grad_gain,
    parts, results, across, arrived, sent,
):
    heads = key.shape[1] // HD
    per_head = suffix.shape[0] // heads
    state_rows = suffix.shape[1] - GAIN_ROWS
    _, cuts, rows, _ = parts.shape
    operands, outputs = (value, key), (grad_key, grad_value)
    order = [(c, n) for c in range(cuts) for n in range(2)]

    def read(c, n):
        source = (key_part, value_part)[n].at[pl.ds(c * rows, rows)]
        return pltpu.make_async_copy(source, parts.at[n, c], arrived.at[n, c])

    def write(c, n):
        target = outputs[n].at[pl.ds(c * rows, rows)]
        return pltpu.make_async_copy(results.at[n, c], target, sent.at[n, c])

    def product(c, n, i):
        state = suffix[i * per_head : (i + 1) * per_head, :state_rows].reshape(HD, HD)
        operand = operands[n][c * rows : (c + 1) * rows, i * HD : (i + 1) * HD]
        return dot(operand, state, 1, 1 - n)

    for c, n in order:
        read(c, n).start()
    for i in range(heads):
        columns = slice(i * HD, (i + 1) * HD)
        tile = suffix[i * per_head, state_rows:].astype(F32)
        grad_gain[:, columns] = jnp.sum(tile, axis=0, keepdims=True)
        for n in range(2):
            across[n, :, columns] = product(0, n, i)
    for c, n in order:
        read(c, n).wait()
        for i in range(heads):
            columns = slice(i * HD, (i + 1) * HD)
            x = across[n, :, columns] if c == 0 else product(c, n, i)
            results[n, c, :, columns] = (parts[n, c, :, columns].astype(F32) + x).astype(BF16)
        write(c, n).start()
    for c, n in order:
        write(c, n).wait()


def exchange(array, axis):
    return lax.all_to_all(array, axis, 0, 0, tiled=True)


def layer(query, key, value, gain, cotangent):
    rows, width = query.shape
    heads = width // HD
    tp, devices = lax.axis_size("tp"), lax.axis_size("seq")
    full_width = tp * width
    piece = width // devices
    gain = gain.reshape(1, width)

    def call(kernel, inputs, outputs, steps, flops=0, scratch=(), mib=60):
        def spec(array, cut):
            shape = list(array.shape)
            if cut == "hbm":
                return pl.BlockSpec(memory_space=pltpu.HBM)
            if isinstance(cut, tuple):
                cut = cut[1]
            if not steps:
                return pl.BlockSpec(memory_space=pltpu.VMEM)
            if cut is None:
                return pl.BlockSpec(tuple(shape), lambda i: (0,) * len(shape))
            shape[cut] //= steps
            return pl.BlockSpec(
                tuple(shape), lambda i: tuple(i if d == cut else 0 for d in range(len(shape)))
            )

        def space(cut):
            name = cut[0] if isinstance(cut, tuple) else cut
            return {"hbm": pltpu.HBM, "vmem": pltpu.VMEM}.get(name)

        arrays = [
            pltpu.with_memory_space_constraint(a, space(cut)) if space(cut) else a
            for a, cut in inputs
        ]
        bytes_moved = sum(a.size * a.dtype.itemsize for a in arrays + [o for o, _ in outputs])
        return pl.pallas_call(
            kernel,
            grid=(steps,) if steps else (),
            in_specs=[spec(*i) for i in inputs],
            out_specs=[spec(*o) for o in outputs],
            out_shape=[
                space(cut)(o.shape, o.dtype) if space(cut) else o for o, cut in outputs
            ],
            scratch_shapes=list(scratch),
            compiler_params=pltpu.CompilerParams(vmem_limit_bytes=mib << 20),
            cost_estimate=pl.CostEstimate(
                flops=flops, bytes_accessed=bytes_moved, transcendentals=0
            ),
        )(*arrays)

    shape = jax.ShapeDtypeStruct
    states = shape((devices, piece, HD), BF16)
    more_states = shape((devices, piece + GAIN_ROWS, HD), BF16)
    wide = shape((rows, width), F32)
    narrow = shape((rows, width), BF16)
    vectors = [pltpu.VMEM((rows, HD), F32)] * 2
    state_flops = 2 * rows * HD * width
    block_flops = 2 * rows * rows * width * 3 // 4

    chunks = 4
    (state,) = call(
        state_kernel, [(key, "hbm"), (value, "hbm")], [(states, None)], 0, state_flops,
        [pltpu.VMEM((chunks, rows // chunks, width), BF16)] * 2
        + [pltpu.VMEM((heads, HD, HD), F32), pltpu.SemaphoreType.DMA((2, chunks))],
    )
    state = exchange(state, "seq")
    (intra,) = call(
        intra_kernel, [(query, 1), (key, 1), (value, 1)], [(wide, ("vmem", 1))],
        heads, 2 * block_flops,
    )
    (prefix,) = call(before_kernel, [(state, None)], [(states, None)], 0, mib=24)
    prefix = exchange(prefix, "seq")
    attended, grads_in, sums = call(
        attend_kernel,
        [(intra, None), (query, None), (prefix, None), (cotangent, "hbm"), (gain, None)],
        [(wide, None), (narrow, ("vmem", None)), (shape((tp, 2 * rows // HD, HD), F32), None)],
        0, state_flops, [pltpu.SemaphoreType.DMA], mib=24,
    )
    sums = exchange(sums, "tp")
    grad_state, again = call(
        functools.partial(out_grad_kernel, full_width),
        [(sums, None), (attended, None), (grads_in, None), (query, None), (gain, None)],
        [(more_states, None), (wide, "hbm")], 0, state_flops,
        [pltpu.SemaphoreType.DMA], mib=24,
    )
    grad_state = exchange(grad_state, "seq")
    normed, grads, grad_query = call(
        functools.partial(query_kernel, full_width),
        [(sums, None), (again, 1), (cotangent, 1), (key, 1), (value, 1), (prefix, 0), (gain, 1)],
        [(narrow, 1), (narrow, 1), (narrow, 1)],
        heads, 2 * block_flops + state_flops, vectors,
    )
    (suffix,) = call(
        after_kernel, [(grad_state, None)],
        [(more_states, None)], 0, mib=48,
    )
    key_part, value_part = call(
        key_value_kernel,
        [(grads, 1), (query, 1), (key, 1), (value, 1)],
        [(narrow, 1), (narrow, 1)],
        heads, 4 * block_flops,
    )
    suffix = exchange(suffix, "seq")
    cuts = 2
    grad_key, grad_value, grad_gain = call(
        last_kernel,
        [(key_part, "hbm"), (value_part, "hbm"), (key, None), (value, None), (suffix, None)],
        [(narrow, "hbm"), (narrow, "hbm"), (shape((1, width), F32), None)],
        0, 2 * state_flops,
        [pltpu.VMEM((2, cuts, rows // cuts, width), BF16)] * 2
        + [pltpu.VMEM((2, rows // cuts, width), F32)]
        + [pltpu.SemaphoreType.DMA((2, cuts))] * 2,
        mib=44,
    )
    return normed, grad_query, grad_key, grad_value, grad_gain.reshape(width)


def solution(mesh):
    block = P("seq", "tp")
    return jax.shard_map(
        layer,
        mesh=mesh,
        in_specs=(block, block, block, P("tp"), block),
        out_specs=(block, block, block, block, P("tp")),
        check_vma=False,
    )
```

```python
import functools

import jax
import jax.numpy as jnp
from jax import lax
from jax.experimental import pallas as pl
from jax.experimental.pallas import tpu as pltpu
from jax.sharding import PartitionSpec as P


HD = 128
EPSILON = 1e-06
GAIN_ROWS = 8
F32, BF16 = jnp.float32, jnp.bfloat16


def dot(a, b, contract_a, contract_b):
    return lax.dot_general(
        a, b, (((contract_a,), (contract_b,)), ((), ())), preferred_element_type=F32
    )


def causal(rows):
    t = lax.broadcasted_iota(jnp.int32, (rows, rows), 0)
    s = lax.broadcasted_iota(jnp.int32, (rows, rows), 1)
    return t >= s


def head(ref, i):
    return ref[:, i * HD : (i + 1) * HD]


def lower_product(a, b, x):
    half = a.shape[0] // 2
    mask = causal(half)
    first, last = slice(0, half), slice(half, None)
    s00 = jnp.where(mask, dot(a[first], b[first], 1, 1), 0.0).astype(BF16)
    s10 = dot(a[last], b[first], 1, 1).astype(BF16)
    s11 = jnp.where(mask, dot(a[last], b[last], 1, 1), 0.0).astype(BF16)
    return dot(s00, x[first], 1, 0), dot(s10, x[first], 1, 0) + dot(s11, x[last], 1, 0)


def upper_product(a, b, x):
    half = a.shape[0] // 2
    s = lax.broadcasted_iota(jnp.int32, (half, half), 0)
    t = lax.broadcasted_iota(jnp.int32, (half, half), 1)
    mask = t >= s
    first, last = slice(0, half), slice(half, None)
    s00 = jnp.where(mask, dot(a[first], b[first], 1, 1), 0.0).astype(BF16)
    s01 = dot(a[first], b[last], 1, 1).astype(BF16)
    s11 = jnp.where(mask, dot(a[last], b[last], 1, 1), 0.0).astype(BF16)
    return dot(s00, x[first], 1, 0) + dot(s01, x[last], 1, 0), dot(s11, x[last], 1, 0)


def three_parts(x):
    high = x.astype(BF16).astype(F32)
    rest = x - high
    middle = rest.astype(BF16).astype(F32)
    return high, middle, rest - middle


def gain_tile(x):
    row = lax.broadcasted_iota(jnp.int32, (GAIN_ROWS, HD), 0)
    high, middle, low = (jnp.broadcast_to(p, (GAIN_ROWS, HD)) for p in three_parts(x))
    tile = jnp.where(row == 0, high, jnp.where(row == 1, middle, jnp.where(row == 2, low, 0.0)))
    return tile.astype(BF16)


def state_kernel(key, value, out, keys, values, total, arrived):
    chunks = keys.shape[0]
    rows = keys.shape[1]
    heads = key.shape[1] // HD
    per_head = out.shape[0] // heads

    def copies(c):
        here = pl.ds(c * rows, rows)
        return (
            pltpu.make_async_copy(key.at[here], keys.at[c], arrived.at[0, c]),
            pltpu.make_async_copy(value.at[here], values.at[c], arrived.at[1, c]),
        )

    for c in range(chunks):
        for copy in copies(c):
            copy.start()
    for c in range(chunks):
        for copy in copies(c):
            copy.wait()
        for i in range(heads):
            here = slice(i * HD, (i + 1) * HD)
            state = dot(keys[c, :, here], values[c, :, here], 0, 0)
            if c > 0:
                state += total[i]
            if c < chunks - 1:
                total[i] = state
            else:
                out[i * per_head : (i + 1) * per_head] = state.astype(BF16).reshape(
                    per_head, -1, HD
                )


def before_kernel(states, out):
    total = jnp.zeros(states.shape[1:], F32)
    for j in range(states.shape[0]):
        out[j] = total.astype(BF16)
        total += states[j].astype(F32)


def after_kernel(states, out):
    devices = states.shape[0]
    rows = states.shape[1] - GAIN_ROWS
    total = jnp.zeros((rows, HD), F32)
    gain = jnp.zeros((GAIN_ROWS, HD), F32)
    for j in reversed(range(devices)):
        out[j, :rows] = total.astype(BF16)
        total += states[j, :rows].astype(F32)
        gain += states[j, rows:].astype(F32)
    tile = gain_tile(jnp.sum(gain, axis=0, keepdims=True))
    for j in range(devices):
        out[j, rows:] = tile


def intra_kernel(query, key, value, out):
    half = query.shape[0] // 2
    for i in range(query.shape[1] // HD):
        top, bottom = lower_product(head(query, i), head(key, i), head(value, i))
        out[:half, i * HD : (i + 1) * HD] = top
        out[half:, i * HD : (i + 1) * HD] = bottom


def attend_kernel(intra, query, prefix, cotangent, gain, attended, grads_in, sums, arrived):
    rows = query.shape[0]
    heads = query.shape[1] // HD
    per_head = prefix.shape[0] // heads
    copy = pltpu.make_async_copy(cotangent, grads_in, arrived)
    copy.start()
    squares = jnp.zeros((rows, HD), F32)
    cross = jnp.zeros((rows, HD), F32)
    for i in range(heads):
        state = prefix[i * per_head : (i + 1) * per_head].reshape(HD, HD)
        att = head(intra, i) + dot(head(query, i), state, 1, 0)
        attended[:, i * HD : (i + 1) * HD] = att
        squares += att * att
    copy.wait()
    for i in range(heads):
        cross += head(attended, i) * (head(grads_in, i).astype(F32) * head(gain, i))
    parts = rows // HD
    for n, x in enumerate((squares, cross)):
        row = jnp.sum(x.T, axis=0, keepdims=True)
        for i in range(parts):
            part = row[:, i * HD : (i + 1) * HD]
            sums[:, n * parts + i, :] = jnp.broadcast_to(part, (sums.shape[0], HD))


def row_factors(sums, full_width):
    total = jnp.sum(sums[...], axis=0)
    parts = total.shape[0] // 2
    inverse, other = [], []
    for i in range(parts):
        sq, cr = total[i : i + 1], total[parts + i : parts + i + 1]
        inv = lax.rsqrt(sq / full_width + EPSILON)
        inverse.append(jnp.broadcast_to(inv, (HD, HD)).T)
        other.append(jnp.broadcast_to(inv * inv * inv * cr / full_width, (HD, HD)).T)
    return jnp.concatenate(inverse, 0), jnp.concatenate(other, 0)


def out_grad_kernel(full_width, sums, attended, cotangent, query, gain, out, again, sent):
    copy = pltpu.make_async_copy(attended, again, sent)
    copy.start()
    heads = query.shape[1] // HD
    per_head = out.shape[0] // heads
    rows = out.shape[1] - GAIN_ROWS
    inv, oth = row_factors(sums, full_width)
    for i in range(heads):
        att, cot = head(attended, i), head(cotangent, i).astype(F32)
        unit = cot * inv
        grad = (unit * head(gain, i) - att * oth).astype(BF16)
        state = dot(head(query, i), grad, 0, 0).astype(BF16)
        here = slice(i * per_head, (i + 1) * per_head)
        out[here, :rows] = state.reshape(per_head, rows, HD)
        tile = gain_tile(jnp.sum(unit * att, axis=0, keepdims=True))
        out[here, rows:] = jnp.broadcast_to(tile[None], (per_head, GAIN_ROWS, HD))
    copy.wait()


def query_kernel(
    full_width, sums, attended, cotangent, key, value, prefix, gain,
    normed, grads, grad_query, inverse, other,
):
    @pl.when(pl.program_id(0) == 0)
    def _():
        inverse[...], other[...] = row_factors(sums, full_width)

    heads = key.shape[1] // HD
    per_head = prefix.shape[0] // heads
    half = key.shape[0] // 2
    inv, oth = inverse[...], other[...]
    for i in range(heads):
        here = slice(i * HD, (i + 1) * HD)
        att, gains = head(attended, i), head(gain, i)
        normed[:, here] = (att * inv * gains).astype(BF16)
        grad = (head(cotangent, i).astype(F32) * inv * gains - att * oth).astype(BF16)
        grads[:, here] = grad
        state = prefix[i * per_head : (i + 1) * per_head].reshape(HD, HD)
        across = dot(grad, state, 1, 1)
        top, bottom = lower_product(grad, head(value, i), head(key, i))
        grad_query[:half, here] = (top + across[:half]).astype(BF16)
        grad_query[half:, here] = (bottom + across[half:]).astype(BF16)


def key_value_kernel(grads, query, key, value, key_part, value_part):
    half = key.shape[0] // 2
    for i in range(key.shape[1] // HD):
        here = slice(i * HD, (i + 1) * HD)
        grad, q = head(grads, i), head(query, i)
        top, bottom = upper_product(head(value, i), grad, q)
        key_part[:half, here] = top.astype(BF16)
        key_part[half:, here] = bottom.astype(BF16)
        top, bottom = upper_product(head(key, i), q, grad)
        value_part[:half, here] = top.astype(BF16)
        value_part[half:, here] = bottom.astype(BF16)


def last_kernel(
    key_part, value_part, key, value, suffix, grad_key, grad_value, grad_gain,
    parts, results, across, arrived, sent,
):
    heads = key.shape[1] // HD
    per_head = suffix.shape[0] // heads
    state_rows = suffix.shape[1] - GAIN_ROWS
    _, cuts, rows, _ = parts.shape
    operands, outputs = (value, key), (grad_key, grad_value)
    order = [(c, n) for c in range(cuts) for n in range(2)]

    def read(c, n):
        source = (key_part, value_part)[n].at[pl.ds(c * rows, rows)]
        return pltpu.make_async_copy(source, parts.at[n, c], arrived.at[n, c])

    def write(c, n):
        target = outputs[n].at[pl.ds(c * rows, rows)]
        return pltpu.make_async_copy(results.at[n, c], target, sent.at[n, c])

    def product(c, n, i):
        state = suffix[i * per_head : (i + 1) * per_head, :state_rows].reshape(HD, HD)
        operand = operands[n][c * rows : (c + 1) * rows, i * HD : (i + 1) * HD]
        return dot(operand, state, 1, 1 - n)

    for c, n in order:
        read(c, n).start()
    for i in range(heads):
        columns = slice(i * HD, (i + 1) * HD)
        tile = suffix[i * per_head, state_rows:].astype(F32)
        grad_gain[:, columns] = jnp.sum(tile, axis=0, keepdims=True)
        for n in range(2):
            across[n, :, columns] = product(0, n, i)
    for c, n in order:
        read(c, n).wait()
        for i in range(heads):
            columns = slice(i * HD, (i + 1) * HD)
            x = across[n, :, columns] if c == 0 else product(c, n, i)
            results[n, c, :, columns] = (parts[n, c, :, columns].astype(F32) + x).astype(BF16)
        write(c, n).start()
    for c, n in order:
        write(c, n).wait()


def exchange(array, axis):
    return lax.all_to_all(array, axis, 0, 0, tiled=True)


def over_heads(array, tp):
    chips = tp // 2
    steps = (
        [(i, i ^ 1) for i in range(tp)],
        [(i, i ^ 2) for i in range(tp)],
        [(i, 2 * (chips - 1 - i // 2) + i % 2) for i in range(tp)],
    )
    for pairs in steps:
        array = array + lax.ppermute(array, "tp", pairs)
    return array


def layer(query, key, value, gain, cotangent):
    rows, width = query.shape
    heads = width // HD
    tp, devices = lax.axis_size("tp"), lax.axis_size("seq")
    full_width = tp * width
    piece = width // devices
    gain = gain.reshape(1, width)

    def call(kernel, inputs, outputs, steps, flops=0, scratch=(), mib=60):
        def spec(array, cut):
            shape = list(array.shape)
            if cut == "hbm":
                return pl.BlockSpec(memory_space=pltpu.HBM)
            if isinstance(cut, tuple):
                cut = cut[1]
            if not steps:
                return pl.BlockSpec(memory_space=pltpu.VMEM)
            if cut is None:
                return pl.BlockSpec(tuple(shape), lambda i: (0,) * len(shape))
            shape[cut] //= steps
            return pl.BlockSpec(
                tuple(shape), lambda i: tuple(i if d == cut else 0 for d in range(len(shape)))
            )

        def space(cut):
            name = cut[0] if isinstance(cut, tuple) else cut
            return {"hbm": pltpu.HBM, "vmem": pltpu.VMEM}.get(name)

        arrays = [
            pltpu.with_memory_space_constraint(a, space(cut)) if space(cut) else a
            for a, cut in inputs
        ]
        bytes_moved = sum(a.size * a.dtype.itemsize for a in arrays + [o for o, _ in outputs])
        return pl.pallas_call(
            kernel,
            grid=(steps,) if steps else (),
            in_specs=[spec(*i) for i in inputs],
            out_specs=[spec(*o) for o in outputs],
            out_shape=[
                space(cut)(o.shape, o.dtype) if space(cut) else o for o, cut in outputs
            ],
            scratch_shapes=list(scratch),
            compiler_params=pltpu.CompilerParams(vmem_limit_bytes=mib << 20),
            cost_estimate=pl.CostEstimate(
                flops=flops, bytes_accessed=bytes_moved, transcendentals=0
            ),
        )(*arrays)

    shape = jax.ShapeDtypeStruct
    states = shape((devices, piece, HD), BF16)
    more_states = shape((devices, piece + GAIN_ROWS, HD), BF16)
    wide = shape((rows, width), F32)
    narrow = shape((rows, width), BF16)
    vectors = [pltpu.VMEM((rows, HD), F32)] * 2
    state_flops = 2 * rows * HD * width
    block_flops = 2 * rows * rows * width * 3 // 4

    chunks = 4
    (state,) = call(
        state_kernel, [(key, "hbm"), (value, "hbm")], [(states, None)], 0, state_flops,
        [pltpu.VMEM((chunks, rows // chunks, width), BF16)] * 2
        + [pltpu.VMEM((heads, HD, HD), F32), pltpu.SemaphoreType.DMA((2, chunks))],
    )
    state = exchange(state, "seq")
    (intra,) = call(
        intra_kernel, [(query, 1), (key, 1), (value, 1)], [(wide, ("vmem", 1))],
        heads, 2 * block_flops,
    )
    (prefix,) = call(before_kernel, [(state, None)], [(states, None)], 0, mib=24)
    prefix = exchange(prefix, "seq")
    attended, grads_in, sums = call(
        attend_kernel,
        [(intra, None), (query, None), (prefix, None), (cotangent, "hbm"), (gain, None)],
        [(wide, None), (narrow, ("vmem", None)), (shape((1, 2 * rows // HD, HD), F32), None)],
        0, state_flops, [pltpu.SemaphoreType.DMA], mib=24,
    )
    sums = over_heads(sums, tp)
    grad_state, again = call(
        functools.partial(out_grad_kernel, full_width),
        [(sums, None), (attended, None), (grads_in, None), (query, None), (gain, None)],
        [(more_states, None), (wide, "hbm")], 0, state_flops,
        [pltpu.SemaphoreType.DMA], mib=24,
    )
    grad_state = exchange(grad_state, "seq")
    normed, grads, grad_query = call(
        functools.partial(query_kernel, full_width),
        [(sums, None), (again, 1), (cotangent, 1), (key, 1), (value, 1), (prefix, 0), (gain, 1)],
        [(narrow, 1), (narrow, 1), (narrow, 1)],
        heads, 2 * block_flops + state_flops, vectors,
    )
    (suffix,) = call(
        after_kernel, [(grad_state, None)],
        [(more_states, None)], 0, mib=48,
    )
    key_part, value_part = call(
        key_value_kernel,
        [(grads, 1), (query, 1), (key, 1), (value, 1)],
        [(narrow, 1), (narrow, 1)],
        heads, 4 * block_flops,
    )
    suffix = exchange(suffix, "seq")
    cuts = 2
    grad_key, grad_value, grad_gain = call(
        last_kernel,
        [(key_part, "hbm"), (value_part, "hbm"), (key, None), (value, None), (suffix, None)],
        [(narrow, "hbm"), (narrow, "hbm"), (shape((1, width), F32), None)],
        0, 2 * state_flops,
        [pltpu.VMEM((2, cuts, rows // cuts, width), BF16)] * 2
        + [pltpu.VMEM((2, rows // cuts, width), F32)]
        + [pltpu.SemaphoreType.DMA((2, cuts))] * 2,
        mib=44,
    )
    return normed, grad_query, grad_key, grad_value, grad_gain.reshape(width)


def solution(mesh):
    block = P("seq", "tp")
    return jax.shard_map(
        layer,
        mesh=mesh,
        in_specs=(block, block, block, P("tp"), block),
        out_specs=(block, block, block, block, P("tp")),
        check_vma=False,
    )
```
